32 devices in a mesh: row: 4 (over z), col: 8 (over y, x, core).
Axes of the slice: x: 2, y: 2, z: 4, core: 2. Of those that a mesh axis runs over, the one named last changes fastest.
Arguments:
- cotangent: float32 [4096, 8192], P('row', 'col'), may hold values from -6 to 6
- whitened: float32 [4096, 8192], P('row', 'col'), may hold values from -0.0625 to 0.0625
- panel_rows: float32 [4, 256, 4096], P(None, None, 'row'), may hold values from -0.375 to 0.375
- diag_inverse: float32 [4, 256, 256], replicated, as said below
Outputs:
- adjoint_rhs: float32 [4096, 8192], P('row', 'col')
- factor_grad: float32 [4, 256, 4096], P(None, 'col', 'row')
The draws below stay inside these ranges and needn't reach their ends.
Inputs may be any that keep to these rules, and one draw needn't show every extreme that they name: `diag_inverse`: each block is lower triangular with diagonal entries between 0.5 and 1.5.
All inputs are finite; a program needn't handle non-finite values.
Results may differ from the reference program's by a relative error of at most 0.00017.
Values sent between devices are 32-bit elements; how exact they have to be, the bound alone decides.
A program may use at most 128 MiB of HBM per device.

```python
import math
import jax
import jax.numpy as jnp
from jax import lax

NB = 256
PANELS = 4
ROWS_DEV = 1024
M = 4096
RHS = 8192
N_ROW = 4


def draw_diag_inverse(key, part):
    first, second = jax.random.split(jax.random.fold_in(key, 17))
    lower = jax.random.normal(first, (PANELS, NB, NB), jnp.float32) / math.sqrt(NB)
    diagonal = jax.random.uniform(second, (PANELS, NB), jnp.float32, 0.5, 1.5)
    return jnp.tril(lower, -1) + diagonal[:, :, None] * jnp.eye(NB, dtype=jnp.float32)[None]


def steps_of(key, extent, cuts, smallest, largest):
    def one(dim, blocks):
        draws = jax.random.uniform(jax.random.fold_in(jax.random.fold_in(key, 6), dim), (blocks,), jnp.float32, smallest / len(cuts), largest / len(cuts))
        return jnp.repeat(jnp.exp(draws), extent[dim] // blocks).reshape((-1,) + (1,) * (len(extent) - dim - 1))

    level = one(*cuts[0])
    for cut in cuts[1:]:
        level = level * one(*cut)
    return level


def centred(own_key, extent, scale, reach, pieces=(), kind=jnp.bfloat16):
    gain = steps_of(own_key, extent, pieces, -0.22, 0.18) if pieces else 1.0
    result = jax.random.normal(own_key, extent, jnp.float32) * scale * gain
    return jnp.minimum(jnp.maximum(result, -reach), reach).astype(kind)


def setup_inputs(seed: int = 0) -> dict:
    key_of = jax.random.split(jax.random.key(seed), 5)
    cotangent = centred(key_of[0], (M, RHS), 1.0, 6.0, ((0, 4), (1, 8)), jnp.float32)
    whitened = centred(key_of[1], (M, RHS), RHS ** -0.5, 0.0625, ((0, 4), (1, 8)), jnp.float32)
    panel_rows = centred(key_of[2], (PANELS, NB, M), NB ** -0.5, 0.375, ((2, 4),), jnp.float32)
    diag_inverse = draw_diag_inverse(jax.random.fold_in(key_of[4], 71), 0)
    return {"cotangent": cotangent, "whitened": whitened, "panel_rows": panel_rows, "diag_inverse": diag_inverse}


def reference(cotangent, whitened, panel_rows, diag_inverse):
    hi = lax.Precision.HIGHEST
    stored = jnp.arange(M, dtype=jnp.int32)
    natural = ((stored % ROWS_DEV) // NB) * N_ROW + stored // ROWS_DEV
    within = stored % NB
    inner = jnp.arange(NB, dtype=jnp.int32)
    blocks = M // NB
    residual = cotangent
    grads = []
    for p in range(PANELS):
        target = blocks - 1 - p
        start = (N_ROW - 1 - p) * ROWS_DEV + ROWS_DEV - NB
        solved = jnp.dot(diag_inverse[p].T, residual[start:start + NB], precision=hi, preferred_element_type=jnp.float32)
        masked = jnp.where((natural < target)[None, :], panel_rows[p], 0.0)
        update = lax.dot_general(masked, solved, (((0,), (0,)), ((), ())), precision=hi, preferred_element_type=jnp.float32)
        residual = residual - update
        residual = jnp.concatenate([residual[:start], solved, residual[start + NB:]], 0)
        term = lax.dot_general(solved, whitened, (((1,), (1,)), ((), ())), precision=hi, preferred_element_type=jnp.float32)
        keep = (natural[None, :] < target) | ((natural[None, :] == target) & (inner[:, None] >= within[None, :]))
        grads.append(-jnp.where(keep, term, 0.0))
    return residual, jnp.stack(grads)
```

```python
import functools

import jax
import jax.numpy as jnp
from jax import lax
from jax.experimental import pallas as pl
from jax.experimental.pallas import tpu as pltpu
from jax.sharding import PartitionSpec as P

MESH = pl.DeviceIdType.MESH
CHUNK = 128
F32 = jnp.float32
BF16 = jnp.bfloat16


def split(x):
    hi = x.astype(BF16)
    return hi, (x - hi.astype(F32)).astype(BF16)


def product(a, b, dims):
    dot = functools.partial(lax.dot_general, dimension_numbers=(dims, ((), ())), preferred_element_type=F32)
    return dot(a[0], b[0]) + (dot(a[0], b[1]) + dot(a[1], b[0]))


NN = ((1,), (0,))
NT = ((1,), (1,))


def kernel(
    n_row, n_col, cot_ref, wht_ref, pan_ref, diag_ref, res_ref, out_ref,
    y, pth, ptl, dth, dtl, wh, wl, grad, rs_buf, recv_sem, down_sem, up_sem, rs_send, rs_recv,
):
    rows, rhs = cot_ref.shape
    panels, width = diag_ref.shape[0], diag_ref.shape[1]
    count = rhs // CHUNK
    blocks = rows // width
    tail = rows - width
    part = width // n_col
    row, col = lax.axis_index("row"), lax.axis_index("col")

    def down(p, c):
        return pltpu.make_async_remote_copy(
            src_ref=y.at[p, c], dst_ref=y.at[p, c], send_sem=down_sem.at[p, c], recv_sem=recv_sem.at[p, c],
            device_id={"row": lax.rem(row + n_row - 1, n_row)}, device_id_type=MESH,
        )

    def up(p, c):
        return pltpu.make_async_remote_copy(
            src_ref=y.at[p, c], dst_ref=y.at[p, c], send_sem=up_sem.at[p, c], recv_sem=recv_sem.at[p, c],
            device_id={"row": lax.rem(row + 1, n_row)}, device_id_type=MESH,
        )

    def scatter(p, j):
        peer = lax.rem(col + j, n_col)
        return pltpu.make_async_remote_copy(
            src_ref=grad.at[p, pl.ds(pl.multiple_of(peer * part, part), part)], dst_ref=rs_buf.at[p, j],
            send_sem=rs_send.at[p, j], recv_sem=rs_recv.at[p, j],
            device_id={"col": peer}, device_id_type=MESH,
        )

    def columns(c):
        return pl.ds(pl.multiple_of(c * CHUNK, CHUNK), CHUNK)

    def solve(p, c, own):
        y[p, c] = product((dth[p], dtl[p]), split(own), NN)

    barrier = pltpu.get_barrier_semaphore()
    for step in (1, n_row - 1):
        pl.semaphore_signal(barrier, inc=1, device_id={"row": lax.rem(row + step, n_row)}, device_id_type=MESH)
    for step in range(1, n_col):
        pl.semaphore_signal(barrier, inc=1, device_id={"col": lax.rem(col + step, n_col)}, device_id_type=MESH)

    @pl.loop(0, panels)
    def _(p):
        hi, lo = split(diag_ref[p].T)
        dth[p] = hi
        dtl[p] = lo

    pl.semaphore_wait(barrier, 2 + n_col - 1)

    @pl.when(row == n_row - 1)
    def _():
        @pl.loop(0, count)
        def _(c):
            solve(0, c, cot_ref[tail:, columns(c)])
            down(0, c).start()

    @pl.loop(0, panels)
    def _(p):
        for b in range(blocks):
            hi, lo = split(pan_ref[p, :, b * width : (b + 1) * width].T)
            pth[p, b * width : (b + 1) * width] = hi
            ptl[p, b * width : (b + 1) * width] = lo
        grad[p] = jnp.zeros(grad.shape[1:], F32)

    @pl.loop(0, count)
    def _(c):
        res_ref[:, columns(c)] = cot_ref[:, columns(c)]
        hi, lo = split(wht_ref[:, columns(c)])
        wh[c] = hi
        wl[c] = lo

    def reduce(p):
        total = grad[p, pl.ds(pl.multiple_of(col * part, part), part)]
        for j in range(1, n_col):
            scatter(p, j).wait_recv()
            total = total + rs_buf[p, j]
        out_ref[p] = total

    @pl.loop(0, panels)
    def _(p):
        root = n_row - 1 - p

        @pl.loop(0, count)
        def _(c):
            @pl.when(row != root)
            def _():
                down(p, c).wait_recv()

            @pl.when((row > root) & (row < n_row - 1))
            def _():
                up(p, c).start()

            @pl.when((row <= root) & (row > 0) & (root < n_row - 1) | (row < root) & (row > 0))
            def _():
                down(p, c).start()

            ys = split(y[p, c])

            @pl.when(row < root)
            def _():
                res_ref[tail:, columns(c)] -= product((pth[p, tail:], ptl[p, tail:]), ys, NN)

                @pl.when((row == root - 1) & (p + 1 < panels))
                def _():
                    solve(p + 1, c, res_ref[tail:, columns(c)])
                    up(p + 1, c).start()

            @pl.when(row == root)
            def _():
                res_ref[tail:, columns(c)] = y[p, c]

            for b in range(blocks - 1):
                at = slice(b * width, (b + 1) * width)
                res_ref[at, columns(c)] -= product((pth[p, at], ptl[p, at]), ys, NN)
            for b in range(blocks):
                at = slice(b * width, (b + 1) * width)
                grad[p, :, at] -= product(ys, (wh[c, at], wl[c, at]), NT)

        inner = lax.broadcasted_iota(jnp.int32, (width, width), 0)
        within = lax.broadcasted_iota(jnp.int32, (width, width), 1)
        keep = (row < root) | ((row == root) & (inner >= within))
        grad[p, :, tail:] = jnp.where(keep, grad[p, :, tail:], 0.0)
        for j in range(1, n_col):
            scatter(p, j).start()

        @pl.when(p > 0)
        def _():
            reduce(p - 1)

    reduce(panels - 1)

    @pl.loop(0, panels)
    def _(p):
        root = n_row - 1 - p
        for j in range(1, n_col):
            scatter(p, j).wait_send()

        @pl.loop(0, count)
        def _(c):
            @pl.when((row >= root) & (row < n_row - 1))
            def _():
                up(p, c).wait_send()

            @pl.when((row <= root) & (row > 0))
            def _():
                down(p, c).wait_send()


def solution(mesh):
    n_row, n_col = mesh.shape["row"], mesh.shape["col"]

    def body(cotangent, whitened, panel_rows, diag_inverse):
        rows, rhs = cotangent.shape
        panels, width = diag_inverse.shape[:2]
        assert panels <= n_row and n_row >= 3
        count = rhs // CHUNK
        vmem = pl.BlockSpec(memory_space=pltpu.VMEM)
        part = width // n_col
        return pl.pallas_call(
            functools.partial(kernel, n_row, n_col),
            out_shape=(
                jax.ShapeDtypeStruct((rows, rhs), F32),
                jax.ShapeDtypeStruct((panels, part, rows), F32),
            ),
            in_specs=[vmem] * 4,
            out_specs=(vmem, vmem),
            scratch_shapes=[
                pltpu.VMEM((panels, count, width, CHUNK), F32),
                pltpu.VMEM((panels, rows, width), BF16),
                pltpu.VMEM((panels, rows, width), BF16),
                pltpu.VMEM((panels, width, width), BF16),
                pltpu.VMEM((panels, width, width), BF16),
                pltpu.VMEM((count, rows, CHUNK), BF16),
                pltpu.VMEM((count, rows, CHUNK), BF16),
                pltpu.VMEM((panels, width, rows), F32),
                pltpu.VMEM((panels, n_col, part, rows), F32),
                pltpu.SemaphoreType.DMA((panels, count)),
                pltpu.SemaphoreType.DMA((panels, count)),
                pltpu.SemaphoreType.DMA((panels, count)),
                pltpu.SemaphoreType.DMA((panels, n_col)),
                pltpu.SemaphoreType.DMA((panels, n_col)),
            ],
            compiler_params=pltpu.CompilerParams(
                collective_id=0, has_side_effects=True, vmem_limit_bytes=60 * 1024 * 1024
            ),
        )(cotangent, whitened, panel_rows, diag_inverse)

    return jax.shard_map(
        body,
        mesh=mesh,
        in_specs=(P("row", "col"), P("row", "col"), P(None, None, "row"), P()),
        out_specs=(P("row", "col"), P(None, "col", "row")),
        check_vma=False,
    )
```

```python
import functools

import jax
import jax.numpy as jnp
from jax import lax
from jax.experimental import pallas as pl
from jax.experimental.pallas import tpu as pltpu
from jax.sharding import PartitionSpec as P

MESH = pl.DeviceIdType.MESH
CHUNK = 128
HALVES = 2
F32 = jnp.float32
BF16 = jnp.bfloat16


def split(x):
    hi = x.astype(BF16)
    return hi, (x - hi.astype(F32)).astype(BF16)


def product(a, b, dims):
    dot = functools.partial(lax.dot_general, dimension_numbers=(dims, ((), ())), preferred_element_type=F32)
    return dot(a[0], b[0]) + (dot(a[0], b[1]) + dot(a[1], b[0]))


NN = ((1,), (0,))
NT = ((1,), (1,))


def kernel(
    n_row, n_col, cot_hbm, wht_hbm, pan_hbm, diag_hbm, res_ref, out_ref,
    wht_ref, pan_ref, diag_ref, y, pth, ptl, dth, dtl, wh, wl, grad, rs_a, rs_b,
    local_sem, recv_sem, down_sem, up_sem, a_send, a_recv, b_send, b_recv,
):
    rows, rhs = res_ref.shape
    panels, width = diag_ref.shape[0], diag_ref.shape[1]
    count = rhs // CHUNK
    blocks = rows // width
    tail = rows - width
    part = width // n_col
    chips = n_col // 2
    half = width // HALVES
    row, col = lax.axis_index("row"), lax.axis_index("col")
    core, chip = lax.rem(col, 2), col // 2

    def y_copy(p, c, h, sems, step):
        block = y.at[p, c, h * half : (h + 1) * half]
        return pltpu.make_async_remote_copy(
            src_ref=block, dst_ref=block, send_sem=sems.at[p, c, h], recv_sem=recv_sem.at[p, c, h],
            device_id={"row": lax.rem(row + step, n_row)}, device_id_type=MESH,
        )

    def down(p, c, h):
        return y_copy(p, c, h, down_sem, n_row - 1)

    def up(p, c, h):
        return y_copy(p, c, h, up_sem, 1)

    def group(g):
        return slice(0, blocks - 1) if g == 0 else slice(blocks - 1, blocks)

    def pair_copy(p, m, g):
        place = (2 * m + 1 - core) * part
        return pltpu.make_async_remote_copy(
            src_ref=grad.at[p, group(g), pl.ds(pl.multiple_of(place, part), part)], dst_ref=rs_a.at[p, m, group(g)],
            send_sem=a_send.at[p, m, g], recv_sem=a_recv.at[p, m, g],
            device_id={"col": 2 * chip + 1 - core}, device_id_type=MESH,
        )

    def chip_copy(p, j, g):
        peer = lax.rem(chip + j, chips)
        return pltpu.make_async_remote_copy(
            src_ref=rs_a.at[p, peer, group(g)], dst_ref=rs_b.at[p, j, group(g)],
            send_sem=b_send.at[p, j, g], recv_sem=b_recv.at[p, j, g],
            device_id={"col": 2 * peer + core}, device_id_type=MESH,
        )

    def groups(p, act):
        act(0)

        @pl.when(row <= n_row - 1 - p)
        def _():
            act(1)

    def pair_start(p):
        def act(g):
            for m in range(chips):
                pair_copy(p, m, g).start()

        groups(p, act)

    def chip_start(p):
        def act(g):
            for m in range(chips):
                pair_copy(p, m, g).wait_recv()
            for m in range(chips):
                place = pl.multiple_of((2 * m + core) * part, part)
                rs_a[p, m, group(g)] += grad[p, group(g), pl.ds(place, part)]
            for j in range(1, chips):
                chip_copy(p, j, g).start()

        groups(p, act)

    def finish(p):
        def act(g):
            for j in range(1, chips):
                chip_copy(p, j, g).wait_recv()
            for b in range(blocks)[group(g)]:
                total = rs_a[p, chip, b]
                for j in range(1, chips):
                    total = total + rs_b[p, j, b]
                out_ref[p, :, b * width : (b + 1) * width] = total

        out_ref[p, :, tail:] = jnp.zeros((part, width), F32)
        groups(p, act)

    def columns(c):
        return pl.ds(pl.multiple_of(c * CHUNK, CHUNK), CHUNK)

    def solve(p, c, own):
        y[p, c] = product((dth[p], dtl[p]), split(own), NN)

    barrier = pltpu.get_barrier_semaphore()
    for step in (1, n_row - 1):
        pl.semaphore_signal(barrier, inc=1, device_id={"row": lax.rem(row + step, n_row)}, device_id_type=MESH)
    for step in range(1, n_col):
        pl.semaphore_signal(barrier, inc=1, device_id={"col": lax.rem(col + step, n_col)}, device_id_type=MESH)

    diag_copy = pltpu.make_async_copy(diag_hbm, diag_ref, local_sem.at[0])
    tail_copy = pltpu.make_async_copy(cot_hbm.at[tail:], res_ref.at[tail:], local_sem.at[1])
    pan_copy = pltpu.make_async_copy(pan_hbm, pan_ref, local_sem.at[2])
    head_copy = pltpu.make_async_copy(cot_hbm.at[:tail], res_ref.at[:tail], local_sem.at[3])
    wht_copy = pltpu.make_async_copy(wht_hbm, wht_ref, local_sem.at[4])
    for copy in (diag_copy, tail_copy, pan_copy, head_copy, wht_copy):
        copy.start()

    diag_copy.wait()

    @pl.loop(0, panels)
    def _(p):
        hi, lo = split(diag_ref[p].T)
        dth[p] = hi
        dtl[p] = lo

    tail_copy.wait()
    pl.semaphore_wait(barrier, 2 + n_col - 1)

    @pl.when(row == n_row - 1)
    def _():
        @pl.loop(0, count)
        def _(c):
            solve(0, c, res_ref[tail:, columns(c)])
            for h in range(HALVES):
                down(0, c, h).start()

    pan_copy.wait()

    @pl.loop(0, panels)
    def _(p):
        for b in range(blocks):
            hi, lo = split(pan_ref[p, :, b * width : (b + 1) * width].T)
            pth[p, b * width : (b + 1) * width] = hi
            ptl[p, b * width : (b + 1) * width] = lo
        grad[p] = jnp.zeros(grad.shape[1:], F32)

    head_copy.wait()
    wht_copy.wait()

    @pl.loop(0, count)
    def _(c):
        hi, lo = split(wht_ref[:, columns(c)])
        wh[c] = hi
        wl[c] = lo

    @pl.loop(0, panels)
    def _(p):
        root = n_row - 1 - p

        @pl.loop(0, count)
        def _(c):
            for h in range(HALVES):
                @pl.when(row != root)
                def _():
                    down(p, c, h).wait_recv()

                @pl.when((row > root) & (row < n_row - 1))
                def _():
                    up(p, c, h).start()

                @pl.when((row > 0) & ((row < root) | ((row == root) & (p > 0))))
                def _():
                    down(p, c, h).start()

            ys = split(y[p, c])

            @pl.when(row < root)
            def _():
                res_ref[tail:, columns(c)] -= product((pth[p, tail:], ptl[p, tail:]), ys, NN)

                @pl.when((row == root - 1) & (p + 1 < panels))
                def _():
                    solve(p + 1, c, res_ref[tail:, columns(c)])
                    for h in range(HALVES):
                        up(p + 1, c, h).start()

            @pl.when(row == root)
            def _():
                res_ref[tail:, columns(c)] = y[p, c]

            for b in range(blocks - 1):
                at = slice(b * width, (b + 1) * width)
                res_ref[at, columns(c)] -= product((pth[p, at], ptl[p, at]), ys, NN)
            for b in range(blocks):
                at = slice(b * width, (b + 1) * width)
                grad[p, b] -= product(ys, (wh[c, at], wl[c, at]), NT)

            @pl.when((c == count // 2) & (p > 0))
            def _():
                chip_start(p - 1)

        @pl.when(row == root)
        def _():
            inner = lax.broadcasted_iota(jnp.int32, (width, width), 0)
            within = lax.broadcasted_iota(jnp.int32, (width, width), 1)
            grad[p, blocks - 1] = jnp.where(inner >= within, grad[p, blocks - 1], 0.0)

        pair_start(p)

        @pl.when(p > 0)
        def _():
            finish(p - 1)

    chip_start(panels - 1)
    finish(panels - 1)

    @pl.loop(0, panels)
    def _(p):
        root = n_row - 1 - p

        def act(g):
            for m in range(chips):
                pair_copy(p, m, g).wait_send()
            for j in range(1, chips):
                chip_copy(p, j, g).wait_send()

        groups(p, act)

        @pl.loop(0, count)
        def _(c):
            for h in range(HALVES):
                @pl.when((row >= root) & (row < n_row - 1))
                def _():
                    up(p, c, h).wait_send()

                @pl.when((row <= root) & (row > 0))
                def _():
                    down(p, c, h).wait_send()


def solution(mesh):
    n_row, n_col = mesh.shape["row"], mesh.shape["col"]

    def body(cotangent, whitened, panel_rows, diag_inverse):
        rows, rhs = cotangent.shape
        panels, width = diag_inverse.shape[:2]
        assert panels <= n_row and n_row >= 3 and n_col % 2 == 0
        count, blocks, part, chips = rhs // CHUNK, rows // width, width // n_col, n_col // 2
        vmem = pl.BlockSpec(memory_space=pltpu.VMEM)
        hbm = pl.BlockSpec(memory_space=pltpu.HBM)
        dma = pltpu.SemaphoreType.DMA
        return pl.pallas_call(
            functools.partial(kernel, n_row, n_col),
            out_shape=(pltpu.VMEM((rows, rhs), F32), pltpu.VMEM((panels, part, rows), F32)),
            in_specs=[hbm] * 4,
            out_specs=(vmem, vmem),
            scratch_shapes=[
                pltpu.VMEM((rows, rhs), F32),
                pltpu.VMEM((panels, width, rows), F32),
                pltpu.VMEM((panels, width, width), F32),
                pltpu.VMEM((panels, count, width, CHUNK), F32),
                pltpu.VMEM((panels, rows, width), BF16),
                pltpu.VMEM((panels, rows, width), BF16),
                pltpu.VMEM((panels, width, width), BF16),
                pltpu.VMEM((panels, width, width), BF16),
                pltpu.VMEM((count, rows, CHUNK), BF16),
                pltpu.VMEM((count, rows, CHUNK), BF16),
                pltpu.VMEM((panels, blocks, width, width), F32),
                pltpu.VMEM((panels, chips, blocks, part, width), F32),
                pltpu.VMEM((panels, chips, blocks, part, width), F32),
                dma((5,)),
                dma((panels, count, HALVES)),
                dma((panels, count, HALVES)),
                dma((panels, count, HALVES)),
                dma((panels, chips, 2)),
                dma((panels, chips, 2)),
                dma((panels, chips, 2)),
                dma((panels, chips, 2)),
            ],
            compiler_params=pltpu.CompilerParams(
                collective_id=0, has_side_effects=True, vmem_limit_bytes=117 * 512 * 1024
            ),
        )(cotangent, whitened, panel_rows, diag_inverse)

    return jax.shard_map(
        body,
        mesh=mesh,
        in_specs=(P("row", "col"), P("row", "col"), P(None, None, "row"), P()),
        out_specs=(P("row", "col"), P(None, "col", "row")),
        check_vma=False,
    )
```

```python
import functools

import jax
import jax.numpy as jnp
from jax import lax
from jax.experimental import pallas as pl
from jax.experimental.pallas import tpu as pltpu
from jax.sharding import PartitionSpec as P

MESH = pl.DeviceIdType.MESH
CHUNK = 128
HALVES = 2
F32 = jnp.float32
BF16 = jnp.bfloat16


def split(x):
    hi = x.astype(BF16)
    return hi, (x - hi.astype(F32)).astype(BF16)


def product(a, b, dims):
    dot = functools.partial(lax.dot_general, dimension_numbers=(dims, ((), ())), preferred_element_type=F32)
    return dot(a[0], b[0]) + (dot(a[0], b[1]) + dot(a[1], b[0]))


NN = ((1,), (0,))
NT = ((1,), (1,))


def kernel(
    n_row, n_col, cot_hbm, wht_hbm, pan_hbm, diag_hbm, res_ref, out_ref,
    wht_ref, pan_ref, diag_ref, y, pth, ptl, dth, dtl, wh, wl, grad, rs_a, rs_b, far_pan, far_own, far_sum, fph, fpl,
    local_sem, recv_sem, down_sem, up_sem, a_send, a_recv, b_send, b_recv, fp_send, fp_recv, fo_send, fo_recv,
):
    rows, rhs = res_ref.shape
    panels, width = diag_ref.shape[0], diag_ref.shape[1]
    count = rhs // CHUNK
    blocks = rows // width
    tail = rows - width
    part = width // n_col
    chips = n_col // 2
    half = width // HALVES
    row, col = lax.axis_index("row"), lax.axis_index("col")
    core, chip = lax.rem(col, 2), col // 2
    last = panels - 1
    last_root = n_row - panels
    helper = last_root + 1

    def y_copy(p, c, h, sems, step):
        block = y.at[p, c, h * half : (h + 1) * half]
        return pltpu.make_async_remote_copy(
            src_ref=block, dst_ref=block, send_sem=sems.at[p, c, h], recv_sem=recv_sem.at[p, c, h],
            device_id={"row": lax.rem(row + step, n_row)}, device_id_type=MESH,
        )

    def down(p, c, h):
        return y_copy(p, c, h, down_sem, n_row - 1)

    def up(p, c, h):
        return y_copy(p, c, h, up_sem, 1)

    def far_panel(p):
        return pltpu.make_async_remote_copy(
            src_ref=pan_hbm.at[p, :, tail:], dst_ref=far_pan.at[p], send_sem=fp_send.at[p], recv_sem=fp_recv.at[p],
            device_id={"row": lax.rem(row + 1, n_row)}, device_id_type=MESH,
        )

    def far_rows(c):
        return pltpu.make_async_remote_copy(
            src_ref=cot_hbm.at[tail:, columns(c)], dst_ref=far_own.at[c], send_sem=fo_send.at[c], recv_sem=fo_recv.at[c],
            device_id={"row": lax.rem(row + 1, n_row)}, device_id_type=MESH,
        )

    def group(g):
        return slice(0, blocks - 1) if g == 0 else slice(blocks - 1, blocks)

    def pair_copy(p, m, g):
        place = (2 * m + 1 - core) * part
        return pltpu.make_async_remote_copy(
            src_ref=grad.at[p, group(g), pl.ds(pl.multiple_of(place, part), part)], dst_ref=rs_a.at[p, m, group(g)],
            send_sem=a_send.at[p, m, g], recv_sem=a_recv.at[p, m, g],
            device_id={"col": 2 * chip + 1 - core}, device_id_type=MESH,
        )

    def chip_copy(p, j, g):
        peer = lax.rem(chip + j, chips)
        return pltpu.make_async_remote_copy(
            src_ref=rs_a.at[p, peer, group(g)], dst_ref=rs_b.at[p, j, group(g)],
            send_sem=b_send.at[p, j, g], recv_sem=b_recv.at[p, j, g],
            device_id={"col": 2 * peer + core}, device_id_type=MESH,
        )

    def groups(p, act):
        act(0)

        @pl.when(row <= n_row - 1 - p)
        def _():
            act(1)

    def pair_start(p):
        def act(g):
            for m in range(chips):
                pair_copy(p, m, g).start()

        groups(p, act)

    def chip_start(p):
        def act(g):
            for m in range(chips):
                pair_copy(p, m, g).wait_recv()
            for m in range(chips):
                place = pl.multiple_of((2 * m + core) * part, part)
                rs_a[p, m, group(g)] += grad[p, group(g), pl.ds(place, part)]
            for j in range(1, chips):
                chip_copy(p, j, g).start()

        groups(p, act)

    def finish(p):
        def act(g):
            for j in range(1, chips):
                chip_copy(p, j, g).wait_recv()
            for b in range(blocks)[group(g)]:
                total = rs_a[p, chip, b]
                for j in range(1, chips):
                    total = total + rs_b[p, j, b]
                out_ref[p, :, b * width : (b + 1) * width] = total

        out_ref[p, :, tail:] = jnp.zeros((part, width), F32)
        groups(p, act)

    def columns(c):
        return pl.ds(pl.multiple_of(c * CHUNK, CHUNK), CHUNK)

    def solve(p, c, own):
        y[p, c] = product((dth[p], dtl[p]), split(own), NN)

    barrier = pltpu.get_barrier_semaphore()
    for step in (1, n_row - 1):
        pl.semaphore_signal(barrier, inc=1, device_id={"row": lax.rem(row + step, n_row)}, device_id_type=MESH)
    for step in range(1, n_col):
        pl.semaphore_signal(barrier, inc=1, device_id={"col": lax.rem(col + step, n_col)}, device_id_type=MESH)

    diag_copy = pltpu.make_async_copy(diag_hbm, diag_ref, local_sem.at[0])
    tail_copy = pltpu.make_async_copy(cot_hbm.at[tail:], res_ref.at[tail:], local_sem.at[1])
    pan_copy = pltpu.make_async_copy(pan_hbm, pan_ref, local_sem.at[2])
    head_copy = pltpu.make_async_copy(cot_hbm.at[:tail], res_ref.at[:tail], local_sem.at[3])
    wht_copy = pltpu.make_async_copy(wht_hbm, wht_ref, local_sem.at[4])
    for copy in (diag_copy, tail_copy, pan_copy, head_copy, wht_copy):
        copy.start()

    diag_copy.wait()

    @pl.loop(0, panels)
    def _(p):
        hi, lo = split(diag_ref[p].T)
        dth[p] = hi
        dtl[p] = lo

    tail_copy.wait()
    pl.semaphore_wait(barrier, 2 + n_col - 1)

    @pl.when(row == n_row - 1)
    def _():
        @pl.loop(0, count)
        def _(c):
            solve(0, c, res_ref[tail:, columns(c)])
            for h in range(HALVES):
                down(0, c, h).start()

    @pl.when(row == last_root)
    def _():
        @pl.loop(0, last)
        def _(p):
            far_panel(p).start()

        @pl.loop(0, count)
        def _(c):
            far_rows(c).start()

    pan_copy.wait()

    @pl.loop(0, panels)
    def _(p):
        for b in range(blocks):
            hi, lo = split(pan_ref[p, :, b * width : (b + 1) * width].T)
            pth[p, b * width : (b + 1) * width] = hi
            ptl[p, b * width : (b + 1) * width] = lo
        grad[p] = jnp.zeros(grad.shape[1:], F32)

    head_copy.wait()
    wht_copy.wait()

    @pl.loop(0, count)
    def _(c):
        hi, lo = split(wht_ref[:, columns(c)])
        wh[c] = hi
        wl[c] = lo

    far_sum[...] = jnp.zeros(far_sum.shape, F32)

    @pl.loop(0, panels)
    def _(p):
        root = n_row - 1 - p

        @pl.when((row == helper) & (p < last))
        def _():
            far_panel(p).wait_recv()
            hi, lo = split(far_pan[p].T)
            fph[...] = hi
            fpl[...] = lo

        @pl.loop(0, count)
        def _(c):
            for h in range(HALVES):
                @pl.when((row != root) & ((p < last) | (row != helper)))
                def _():
                    down(p, c, h).wait_recv()

                @pl.when((row > root) & (row < n_row - 1) & ((p < last) | (row != helper)))
                def _():
                    up(p, c, h).start()

                @pl.when((row > 0) & ((row < root) | ((row == root) & (p > 0))))
                def _():
                    down(p, c, h).start()

            ys = split(y[p, c])

            @pl.when(row < root)
            def _():
                res_ref[tail:, columns(c)] -= product((pth[p, tail:], ptl[p, tail:]), ys, NN)

                @pl.when((row == root - 1) & (p + 1 < panels))
                def _():
                    solve(p + 1, c, res_ref[tail:, columns(c)])

                    @pl.when(p + 1 < last)
                    def _():
                        for h in range(HALVES):
                            up(p + 1, c, h).start()

            @pl.when((row == helper) & (p < last))
            def _():
                far_sum[c] += product((fph[...], fpl[...]), ys, NN)

                @pl.when(p == last - 1)
                def _():
                    far_rows(c).wait_recv()
                    solve(last, c, far_own[c] - far_sum[c])
                    for h in range(HALVES):
                        up(last, c, h).start()

            @pl.when(row == root)
            def _():
                res_ref[tail:, columns(c)] = y[p, c]

            for b in range(blocks - 1):
                at = slice(b * width, (b + 1) * width)
                res_ref[at, columns(c)] -= product((pth[p, at], ptl[p, at]), ys, NN)
            for b in range(blocks):
                at = slice(b * width, (b + 1) * width)
                grad[p, b] -= product(ys, (wh[c, at], wl[c, at]), NT)

            @pl.when((c == count // 2) & (p > 0))
            def _():
                chip_start(p - 1)

        @pl.when(row == root)
        def _():
            inner = lax.broadcasted_iota(jnp.int32, (width, width), 0)
            within = lax.broadcasted_iota(jnp.int32, (width, width), 1)
            grad[p, blocks - 1] = jnp.where(inner >= within, grad[p, blocks - 1], 0.0)

        pair_start(p)

        @pl.when(p > 0)
        def _():
            finish(p - 1)

    chip_start(panels - 1)
    finish(panels - 1)

    @pl.loop(0, panels)
    def _(p):
        root = n_row - 1 - p

        def act(g):
            for m in range(chips):
                pair_copy(p, m, g).wait_send()
            for j in range(1, chips):
                chip_copy(p, j, g).wait_send()

        groups(p, act)

        @pl.loop(0, count)
        def _(c):
            for h in range(HALVES):
                @pl.when((row >= root) & (row < n_row - 1) & ((p < last) | (row > last_root)))
                def _():
                    up(p, c, h).wait_send()

                @pl.when((row <= root) & (row > 0))
                def _():
                    down(p, c, h).wait_send()

    @pl.when(row == last_root)
    def _():
        @pl.loop(0, last)
        def _(p):
            far_panel(p).wait_send()

        @pl.loop(0, count)
        def _(c):
            far_rows(c).wait_send()


def solution(mesh):
    n_row, n_col = mesh.shape["row"], mesh.shape["col"]

    def body(cotangent, whitened, panel_rows, diag_inverse):
        rows, rhs = cotangent.shape
        panels, width = diag_inverse.shape[:2]
        assert 3 <= panels <= n_row and n_col % 2 == 0
        count, blocks, part, chips = rhs // CHUNK, rows // width, width // n_col, n_col // 2
        vmem = pl.BlockSpec(memory_space=pltpu.VMEM)
        hbm = pl.BlockSpec(memory_space=pltpu.HBM)
        dma = pltpu.SemaphoreType.DMA
        return pl.pallas_call(
            functools.partial(kernel, n_row, n_col),
            out_shape=(pltpu.VMEM((rows, rhs), F32), pltpu.VMEM((panels, part, rows), F32)),
            in_specs=[hbm] * 4,
            out_specs=(vmem, vmem),
            scratch_shapes=[
                pltpu.VMEM((rows, rhs), F32),
                pltpu.VMEM((panels, width, rows), F32),
                pltpu.VMEM((panels, width, width), F32),
                pltpu.VMEM((panels, count, width, CHUNK), F32),
                pltpu.VMEM((panels, rows, width), BF16),
                pltpu.VMEM((panels, rows, width), BF16),
                pltpu.VMEM((panels, width, width), BF16),
                pltpu.VMEM((panels, width, width), BF16),
                pltpu.VMEM((count, rows, CHUNK), BF16),
                pltpu.VMEM((count, rows, CHUNK), BF16),
                pltpu.VMEM((panels, blocks, width, width), F32),
                pltpu.VMEM((panels, chips, blocks, part, width), F32),
                pltpu.VMEM((panels, chips, blocks, part, width), F32),
                pltpu.VMEM((panels - 1, width, width), F32),
                pltpu.VMEM((count, width, CHUNK), F32),
                pltpu.VMEM((count, width, CHUNK), F32),
                pltpu.VMEM((width, width), BF16),
                pltpu.VMEM((width, width), BF16),
                dma((5,)),
                dma((panels, count, HALVES)),
                dma((panels, count, HALVES)),
                dma((panels, count, HALVES)),
                dma((panels, chips, 2)),
                dma((panels, chips, 2)),
                dma((panels, chips, 2)),
                dma((panels, chips, 2)),
                dma((panels - 1,)),
                dma((panels - 1,)),
                dma((count,)),
                dma((count,)),
            ],
            compiler_params=pltpu.CompilerParams(
                collective_id=0, has_side_effects=True, vmem_limit_bytes=117 * 512 * 1024
            ),
        )(cotangent, whitened, panel_rows, diag_inverse)

    return jax.shard_map(
        body,
        mesh=mesh,
        in_specs=(P("row", "col"), P("row", "col"), P(None, None, "row"), P()),
        out_specs=(P("row", "col"), P(None, "col", "row")),
        check_vma=False,
    )
```

```python
import functools

import jax
import jax.numpy as jnp
from jax import lax
from jax.experimental import pallas as pl
from jax.experimental.pallas import tpu as pltpu
from jax.sharding import PartitionSpec as P

MESH = pl.DeviceIdType.MESH
CHUNK = 128
HALVES = 2
F32 = jnp.float32
BF16 = jnp.bfloat16


def split(x):
    hi = x.astype(BF16)
    return hi, (x - hi.astype(F32)).astype(BF16)


def product(a, b, dims):
    dot = functools.partial(lax.dot_general, dimension_numbers=(dims, ((), ())), preferred_element_type=F32)
    return dot(a[0], b[0]) + (dot(a[0], b[1]) + dot(a[1], b[0]))


NN = ((1,), (0,))
NT = ((1,), (1,))


def kernel(
    n_row, n_col, cot_hbm, wht_hbm, pan_hbm, diag_hbm, res_ref, out_ref,
    wht_ref, pan_ref, diag_ref, y, pth, ptl, dth, dtl, wh, wl, grad, rs_a, rs_b, far_pan, far_own, far_sum, fph, fpl,
    local_sem, recv_sem, down_sem, up_sem, a_send, a_recv, b_send, b_recv, fp_send, fp_recv, fo_send, fo_recv,
):
    rows, rhs = res_ref.shape
    panels, width = diag_ref.shape[0], diag_ref.shape[1]
    count = rhs // CHUNK
    blocks = rows // width
    tail = rows - width
    part = width // n_col
    chips = n_col // 2
    half = width // HALVES
    row, col = lax.axis_index("row"), lax.axis_index("col")
    core, chip = lax.rem(col, 2), col // 2
    last = panels - 1
    last_root = n_row - panels
    helper = last_root + 1

    def y_copy(p, c, h, sems, step):
        block = y.at[p, c, h * half : (h + 1) * half]
        return pltpu.make_async_remote_copy(
            src_ref=block, dst_ref=block, send_sem=sems.at[p, c, h], recv_sem=recv_sem.at[p, c, h],
            device_id={"row": lax.rem(row + step, n_row)}, device_id_type=MESH,
        )

    def down(p, c, h):
        return y_copy(p, c, h, down_sem, n_row - 1)

    def up(p, c, h):
        return y_copy(p, c, h, up_sem, 1)

    def far_panel(p):
        return pltpu.make_async_remote_copy(
            src_ref=pan_hbm.at[p, :, tail:], dst_ref=far_pan.at[p], send_sem=fp_send.at[p], recv_sem=fp_recv.at[p],
            device_id={"row": lax.rem(row + 1, n_row)}, device_id_type=MESH,
        )

    def far_rows(c):
        return pltpu.make_async_remote_copy(
            src_ref=cot_hbm.at[tail:, columns(c)], dst_ref=far_own.at[c], send_sem=fo_send.at[c], recv_sem=fo_recv.at[c],
            device_id={"row": lax.rem(row + 1, n_row)}, device_id_type=MESH,
        )

    def group(g):
        return slice(0, blocks - 1) if g == 0 else slice(blocks - 1, blocks)

    def pair_copy(p, m, g):
        place = (2 * m + 1 - core) * part
        return pltpu.make_async_remote_copy(
            src_ref=grad.at[p, group(g), pl.ds(pl.multiple_of(place, part), part)], dst_ref=rs_a.at[p, m, group(g)],
            send_sem=a_send.at[p, m, g], recv_sem=a_recv.at[p, m, g],
            device_id={"col": 2 * chip + 1 - core}, device_id_type=MESH,
        )

    def chip_copy(p, j, g):
        peer = lax.rem(chip + j, chips)
        return pltpu.make_async_remote_copy(
            src_ref=rs_a.at[p, peer, group(g)], dst_ref=rs_b.at[p, j, group(g)],
            send_sem=b_send.at[p, j, g], recv_sem=b_recv.at[p, j, g],
            device_id={"col": 2 * peer + core}, device_id_type=MESH,
        )

    def groups(p, act):
        act(0)

        @pl.when(row <= n_row - 1 - p)
        def _():
            act(1)

    def pair_start(p):
        def act(g):
            for m in range(chips):
                pair_copy(p, m, g).start()

        groups(p, act)

    def chip_start(p):
        def act(g):
            for m in range(chips):
                pair_copy(p, m, g).wait_recv()
            for m in range(chips):
                place = pl.multiple_of((2 * m + core) * part, part)
                rs_a[p, m, group(g)] += grad[p, group(g), pl.ds(place, part)]
            for j in range(1, chips):
                chip_copy(p, j, g).start()

        groups(p, act)

    def finish(p):
        def act(g):
            for j in range(1, chips):
                chip_copy(p, j, g).wait_recv()
            for b in range(blocks)[group(g)]:
                total = rs_a[p, chip, b]
                for j in range(1, chips):
                    total = total + rs_b[p, j, b]
                out_ref[p, :, b * width : (b + 1) * width] = total

        out_ref[p, :, tail:] = jnp.zeros((part, width), F32)
        groups(p, act)

    def columns(c):
        return pl.ds(pl.multiple_of(c * CHUNK, CHUNK), CHUNK)

    def solve(p, c, own):
        y[p, c] = product((dth[p], dtl[p]), split(own), NN)

    barrier = pltpu.get_barrier_semaphore()
    for step in (1, n_row - 1):
        pl.semaphore_signal(barrier, inc=1, device_id={"row": lax.rem(row + step, n_row)}, device_id_type=MESH)
    for step in range(1, n_col):
        pl.semaphore_signal(barrier, inc=1, device_id={"col": lax.rem(col + step, n_col)}, device_id_type=MESH)

    diag_copy = pltpu.make_async_copy(diag_hbm, diag_ref, local_sem.at[0])
    tail_copy = pltpu.make_async_copy(cot_hbm.at[tail:], res_ref.at[tail:], local_sem.at[1])
    pan_copy = pltpu.make_async_copy(pan_hbm, pan_ref, local_sem.at[2])
    head_copy = pltpu.make_async_copy(cot_hbm.at[:tail], res_ref.at[:tail], local_sem.at[3])
    wht_copy = pltpu.make_async_copy(wht_hbm, wht_ref, local_sem.at[4])
    def inverse(p):
        hi, lo = split(diag_ref[p].T)
        dth[p] = hi
        dtl[p] = lo

    diag_copy.start()
    tail_copy.start()
    diag_copy.wait()
    inverse(0)
    tail_copy.wait()
    pl.semaphore_wait(barrier, 2 + n_col - 1)

    @pl.when(row == n_row - 1)
    def _():
        @pl.loop(0, count)
        def _(c):
            solve(0, c, res_ref[tail:, columns(c)])
            for h in range(HALVES):
                down(0, c, h).start()

    @pl.when(row == last_root)
    def _():
        @pl.loop(0, last)
        def _(p):
            far_panel(p).start()

        @pl.loop(0, count)
        def _(c):
            far_rows(c).start()

    for copy in (pan_copy, wht_copy, head_copy):
        copy.start()

    @pl.loop(1, panels)
    def _(p):
        inverse(p)

    pan_copy.wait()

    @pl.loop(0, panels)
    def _(p):
        for b in range(blocks):
            hi, lo = split(pan_ref[p, :, b * width : (b + 1) * width].T)
            pth[p, b * width : (b + 1) * width] = hi
            ptl[p, b * width : (b + 1) * width] = lo
        grad[p] = jnp.zeros(grad.shape[1:], F32)

    head_copy.wait()
    wht_copy.wait()

    @pl.loop(0, count)
    def _(c):
        hi, lo = split(wht_ref[:, columns(c)])
        wh[c] = hi
        wl[c] = lo

    far_sum[...] = jnp.zeros(far_sum.shape, F32)

    @pl.loop(0, panels)
    def _(p):
        root = n_row - 1 - p

        @pl.when((row == helper) & (p < last))
        def _():
            far_panel(p).wait_recv()
            hi, lo = split(far_pan[p].T)
            fph[...] = hi
            fpl[...] = lo

        @pl.loop(0, count)
        def _(c):
            for h in range(HALVES):
                @pl.when((row != root) & ((p < last) | (row != helper)))
                def _():
                    down(p, c, h).wait_recv()

                @pl.when((row > root) & (row < n_row - 1) & ((p < last) | (row != helper)))
                def _():
                    up(p, c, h).start()

                @pl.when((row > 0) & ((row < root) | ((row == root) & (p > 0))))
                def _():
                    down(p, c, h).start()

            ys = split(y[p, c])

            @pl.when(row < root)
            def _():
                res_ref[tail:, columns(c)] -= product((pth[p, tail:], ptl[p, tail:]), ys, NN)

                @pl.when((row == root - 1) & (p + 1 < panels))
                def _():
                    solve(p + 1, c, res_ref[tail:, columns(c)])

                    @pl.when(p + 1 < last)
                    def _():
                        for h in range(HALVES):
                            up(p + 1, c, h).start()

            @pl.when((row == helper) & (p < last))
            def _():
                far_sum[c] += product((fph[...], fpl[...]), ys, NN)

                @pl.when(p == last - 1)
                def _():
                    far_rows(c).wait_recv()
                    solve(last, c, far_own[c] - far_sum[c])
                    for h in range(HALVES):
                        up(last, c, h).start()

            @pl.when(row == root)
            def _():
                res_ref[tail:, columns(c)] = y[p, c]

            begin = jnp.where((row == last_root) & (p == last), panels, p)
            end = jnp.where((row == last_root) & (p == last - 1), panels, p + 1)

            @pl.loop(begin, end)
            def _(q):
                yq = split(y[q, c])
                for b in range(blocks - 1):
                    at = slice(b * width, (b + 1) * width)
                    res_ref[at, columns(c)] -= product((pth[q, at], ptl[q, at]), yq, NN)
                for b in range(blocks):
                    at = slice(b * width, (b + 1) * width)
                    grad[q, b] -= product(yq, (wh[c, at], wl[c, at]), NT)

            @pl.when((c == count // 2) & (p > 0))
            def _():
                chip_start(p - 1)

        @pl.when(row == root)
        def _():
            inner = lax.broadcasted_iota(jnp.int32, (width, width), 0)
            within = lax.broadcasted_iota(jnp.int32, (width, width), 1)
            grad[p, blocks - 1] = jnp.where(inner >= within, grad[p, blocks - 1], 0.0)

        pair_start(p)

        @pl.when((p > 0) & (p < last))
        def _():
            finish(p - 1)

    chip_start(last)
    finish(last - 1)
    finish(last)

    @pl.loop(0, panels)
    def _(p):
        root = n_row - 1 - p

        def act(g):
            for m in range(chips):
                pair_copy(p, m, g).wait_send()
            for j in range(1, chips):
                chip_copy(p, j, g).wait_send()

        groups(p, act)

        @pl.loop(0, count)
        def _(c):
            for h in range(HALVES):
                @pl.when((row >= root) & (row < n_row - 1) & ((p < last) | (row > last_root)))
                def _():
                    up(p, c, h).wait_send()

                @pl.when((row <= root) & (row > 0))
                def _():
                    down(p, c, h).wait_send()

    @pl.when(row == last_root)
    def _():
        @pl.loop(0, last)
        def _(p):
            far_panel(p).wait_send()

        @pl.loop(0, count)
        def _(c):
            far_rows(c).wait_send()


def store_kernel(res_ref, grad_ref, res_hbm, grad_hbm, sems):
    copies = (
        pltpu.make_async_copy(res_ref, res_hbm, sems.at[0]),
        pltpu.make_async_copy(grad_ref, grad_hbm, sems.at[1]),
    )
    for copy in copies:
        copy.start()
    for copy in copies:
        copy.wait()


def solution(mesh):
    n_row, n_col = mesh.shape["row"], mesh.shape["col"]

    def body(cotangent, whitened, panel_rows, diag_inverse):
        rows, rhs = cotangent.shape
        panels, width = diag_inverse.shape[:2]
        assert 3 <= panels <= n_row and n_col % 2 == 0
        count, blocks, part, chips = rhs // CHUNK, rows // width, width // n_col, n_col // 2
        vmem = pl.BlockSpec(memory_space=pltpu.VMEM)
        hbm = pl.BlockSpec(memory_space=pltpu.HBM)
        dma = pltpu.SemaphoreType.DMA
        kept = pl.pallas_call(
            functools.partial(kernel, n_row, n_col),
            out_shape=(pltpu.VMEM((rows, rhs), F32), pltpu.VMEM((panels, part, rows), F32)),
            in_specs=[hbm] * 4,
            out_specs=(vmem, vmem),
            scratch_shapes=[
                pltpu.VMEM((rows, rhs), F32),
                pltpu.VMEM((panels, width, rows), F32),
                pltpu.VMEM((panels, width, width), F32),
                pltpu.VMEM((panels, count, width, CHUNK), F32),
                pltpu.VMEM((panels, rows, width), BF16),
                pltpu.VMEM((panels, rows, width), BF16),
                pltpu.VMEM((panels, width, width), BF16),
                pltpu.VMEM((panels, width, width), BF16),
                pltpu.VMEM((count, rows, CHUNK), BF16),
                pltpu.VMEM((count, rows, CHUNK), BF16),
                pltpu.VMEM((panels, blocks, width, width), F32),
                pltpu.VMEM((panels, chips, blocks, part, width), F32),
                pltpu.VMEM((panels, chips, blocks, part, width), F32),
                pltpu.VMEM((panels - 1, width, width), F32),
                pltpu.VMEM((count, width, CHUNK), F32),
                pltpu.VMEM((count, width, CHUNK), F32),
                pltpu.VMEM((width, width), BF16),
                pltpu.VMEM((width, width), BF16),
                dma((5,)),
                dma((panels, count, HALVES)),
                dma((panels, count, HALVES)),
                dma((panels, count, HALVES)),
                dma((panels, chips, 2)),
                dma((panels, chips, 2)),
                dma((panels, chips, 2)),
                dma((panels, chips, 2)),
                dma((panels - 1,)),
                dma((panels - 1,)),
                dma((count,)),
                dma((count,)),
            ],
            compiler_params=pltpu.CompilerParams(
                collective_id=0, has_side_effects=True, vmem_limit_bytes=117 * 512 * 1024
            ),
        )(cotangent, whitened, panel_rows, diag_inverse)
        return pl.pallas_call(
            store_kernel,
            out_shape=tuple(jax.ShapeDtypeStruct(k.shape, F32) for k in kept),
            in_specs=[pl.BlockSpec(memory_space=pl.ANY)] * 2,
            out_specs=(hbm, hbm),
            scratch_shapes=[dma((2,))],
            compiler_params=pltpu.CompilerParams(vmem_limit_bytes=1024 * 1024),
        )(*kept)

    return jax.shard_map(
        body,
        mesh=mesh,
        in_specs=(P("row", "col"), P("row", "col"), P(None, None, "row"), P()),
        out_specs=(P("row", "col"), P(None, "col", "row")),
        check_vma=False,
    )
```

```python
import functools

import jax
import jax.numpy as jnp
from jax import lax
from jax.experimental import pallas as pl
from jax.experimental.pallas import tpu as pltpu
from jax.sharding import PartitionSpec as P

MESH = pl.DeviceIdType.MESH
CHUNK = 128
HALVES = 2
F32 = jnp.float32
BF16 = jnp.bfloat16


def split(x):
    hi = x.astype(BF16)
    return hi, (x - hi.astype(F32)).astype(BF16)


def product(a, b, dims):
    dot = functools.partial(lax.dot_general, dimension_numbers=(dims, ((), ())), preferred_element_type=F32)
    return dot(a[0], b[0]) + (dot(a[0], b[1]) + dot(a[1], b[0]))


NN = ((1,), (0,))
NT = ((1,), (1,))


def kernel(
    n_row, n_col, cot_hbm, wht_hbm, pan_hbm, diag_hbm, res_ref, out_ref,
    wht_ref, pan_ref, diag_ref, y, pth, ptl, dth, dtl, wh, wl, grad, rs_a, rs_b, far_pan, far_own, far_sum, fph, fpl,
    local_sem, recv_sem, down_sem, up_sem, a_send, a_recv, b_send, b_recv, fp_send, fp_recv, fo_send, fo_recv,
):
    rows, rhs = res_ref.shape
    panels, width = diag_ref.shape[0], diag_ref.shape[1]
    count = rhs // CHUNK
    blocks = rows // width
    tail = rows - width
    part = width // n_col
    chips = n_col // 2
    half = width // HALVES
    row, col = lax.axis_index("row"), lax.axis_index("col")
    core, chip = lax.rem(col, 2), col // 2
    last = panels - 1
    last_root = n_row - panels
    helper = last_root + 1

    def y_copy(p, c, h, sems, step):
        block = y.at[p, c, h * half : (h + 1) * half]
        return pltpu.make_async_remote_copy(
            src_ref=block, dst_ref=block, send_sem=sems.at[p, c, h], recv_sem=recv_sem.at[p, c, h],
            device_id={"row": lax.rem(row + step, n_row)}, device_id_type=MESH,
        )

    def down(p, c, h):
        return y_copy(p, c, h, down_sem, n_row - 1)

    def up(p, c, h):
        return y_copy(p, c, h, up_sem, 1)

    def far_panel(p):
        return pltpu.make_async_remote_copy(
            src_ref=pan_hbm.at[p, :, tail:], dst_ref=far_pan.at[p], send_sem=fp_send.at[p], recv_sem=fp_recv.at[p],
            device_id={"row": lax.rem(row + 1, n_row)}, device_id_type=MESH,
        )

    def far_rows(c):
        return pltpu.make_async_remote_copy(
            src_ref=cot_hbm.at[tail:, columns(c)], dst_ref=far_own.at[c], send_sem=fo_send.at[c], recv_sem=fo_recv.at[c],
            device_id={"row": lax.rem(row + 1, n_row)}, device_id_type=MESH,
        )

    def group(g):
        return slice(0, blocks - 1) if g == 0 else slice(blocks - 1, blocks)

    def pair_copy(p, m, g):
        place = (2 * m + 1 - core) * part
        return pltpu.make_async_remote_copy(
            src_ref=grad.at[p, group(g), pl.ds(pl.multiple_of(place, part), part)], dst_ref=rs_a.at[p, m, group(g)],
            send_sem=a_send.at[p, m, g], recv_sem=a_recv.at[p, m, g],
            device_id={"col": 2 * chip + 1 - core}, device_id_type=MESH,
        )

    def chip_copy(p, j, g):
        peer = lax.rem(chip + j, chips)
        return pltpu.make_async_remote_copy(
            src_ref=rs_a.at[p, peer, group(g)], dst_ref=rs_b.at[p, j, group(g)],
            send_sem=b_send.at[p, j, g], recv_sem=b_recv.at[p, j, g],
            device_id={"col": 2 * peer + core}, device_id_type=MESH,
        )

    def groups(p, act):
        act(0)

        @pl.when(row <= n_row - 1 - p)
        def _():
            act(1)

    def pair_start(p):
        def act(g):
            for m in range(chips):
                pair_copy(p, m, g).start()

        groups(p, act)

    def chip_start(p):
        def act(g):
            for m in range(chips):
                pair_copy(p, m, g).wait_recv()
            for m in range(chips):
                place = pl.multiple_of((2 * m + core) * part, part)
                rs_a[p, m, group(g)] += grad[p, group(g), pl.ds(place, part)]
            for j in range(1, chips):
                chip_copy(p, j, g).start()

        groups(p, act)

    def finish(p):
        def act(g):
            for j in range(1, chips):
                chip_copy(p, j, g).wait_recv()
            for b in range(blocks)[group(g)]:
                total = rs_a[p, chip, b]
                for j in range(1, chips):
                    total = total + rs_b[p, j, b]
                out_ref[p, :, b * width : (b + 1) * width] = total

        out_ref[p, :, tail:] = jnp.zeros((part, width), F32)
        groups(p, act)

    def columns(c):
        return pl.ds(pl.multiple_of(c * CHUNK, CHUNK), CHUNK)

    def solve(p, c, own):
        y[p, c] = product((dth[p], dtl[p]), split(own), NN)

    barrier = pltpu.get_barrier_semaphore()
    for step in (1, n_row - 1):
        pl.semaphore_signal(barrier, inc=1, device_id={"row": lax.rem(row + step, n_row)}, device_id_type=MESH)
    for step in range(1, n_col):
        pl.semaphore_signal(barrier, inc=1, device_id={"col": lax.rem(col + step, n_col)}, device_id_type=MESH)

    diag_copy = pltpu.make_async_copy(diag_hbm, diag_ref, local_sem.at[0])
    tail_copy = pltpu.make_async_copy(cot_hbm.at[tail:], res_ref.at[tail:], local_sem.at[1])
    pan_copy = pltpu.make_async_copy(pan_hbm, pan_ref, local_sem.at[2])
    head_copy = pltpu.make_async_copy(cot_hbm.at[:tail], res_ref.at[:tail], local_sem.at[3])
    wht_copy = pltpu.make_async_copy(wht_hbm, wht_ref, local_sem.at[4])
    def inverse(p):
        hi, lo = split(diag_ref[p].T)
        dth[p] = hi
        dtl[p] = lo

    diag_copy.start()
    tail_copy.start()
    diag_copy.wait()
    inverse(0)
    tail_copy.wait()
    pl.semaphore_wait(barrier, 2 + n_col - 1)

    @pl.when(row == n_row - 1)
    def _():
        @pl.loop(0, count)
        def _(c):
            solve(0, c, res_ref[tail:, columns(c)])
            for h in range(HALVES):
                down(0, c, h).start()

    @pl.when(row == last_root)
    def _():
        @pl.loop(0, last)
        def _(p):
            far_panel(p).start()

        @pl.loop(0, count)
        def _(c):
            far_rows(c).start()

    for copy in (pan_copy, wht_copy, head_copy):
        copy.start()

    @pl.loop(1, panels)
    def _(p):
        inverse(p)

    pan_copy.wait()

    @pl.loop(0, panels)
    def _(p):
        for b in range(blocks):
            hi, lo = split(pan_ref[p, :, b * width : (b + 1) * width].T)
            pth[p, b * width : (b + 1) * width] = hi
            ptl[p, b * width : (b + 1) * width] = lo
        grad[p] = jnp.zeros(grad.shape[1:], F32)

    head_copy.wait()
    wht_copy.wait()

    @pl.loop(0, count)
    def _(c):
        hi, lo = split(wht_ref[:, columns(c)])
        wh[c] = hi
        wl[c] = lo

    far_sum[...] = jnp.zeros(far_sum.shape, F32)

    @pl.loop(0, panels)
    def _(p):
        root = n_row - 1 - p

        @pl.when((row == helper) & (p < last))
        def _():
            far_panel(p).wait_recv()
            hi, lo = split(far_pan[p].T)
            fph[...] = hi
            fpl[...] = lo

        @pl.loop(0, count)
        def _(c):
            for h in range(HALVES):
                @pl.when((row != root) & ((p < last) | (row != helper)))
                def _():
                    down(p, c, h).wait_recv()

                @pl.when((row > root) & (row < n_row - 1) & ((p < last) | (row != helper)))
                def _():
                    up(p, c, h).start()

                @pl.when((row > 0) & (row < root))
                def _():
                    down(p, c, h).start()

            next_root = (row == root - 1) & (p < last)

            @pl.when(next_root & (row > 0) & (c == count - 1))
            def _():
                @pl.loop(0, count - 1)
                def _(k):
                    for h in range(HALVES):
                        down(p + 1, k, h).start()

            ys = split(y[p, c])

            @pl.when(row < root)
            def _():
                res_ref[tail:, columns(c)] -= product((pth[p, tail:], ptl[p, tail:]), ys, NN)

                @pl.when(next_root)
                def _():
                    solve(p + 1, c, res_ref[tail:, columns(c)])

                    @pl.when((row > 0) & (c == count - 1))
                    def _():
                        for h in range(HALVES):
                            down(p + 1, c, h).start()

                    @pl.when(p + 1 < last)
                    def _():
                        for h in range(HALVES):
                            up(p + 1, c, h).start()

            @pl.when((row == helper) & (p < last))
            def _():
                far_sum[c] += product((fph[...], fpl[...]), ys, NN)

                @pl.when(p == last - 1)
                def _():
                    far_rows(c).wait_recv()
                    solve(last, c, far_own[c] - far_sum[c])
                    for h in range(HALVES):
                        up(last, c, h).start()

            @pl.when(row == root)
            def _():
                res_ref[tail:, columns(c)] = y[p, c]

            begin = jnp.where((row == last_root) & (p == last), panels, p)
            end = jnp.where((row == last_root) & (p == last - 1), panels, p + 1)

            @pl.loop(begin, end)
            def _(q):
                yq = split(y[q, c])
                for b in range(blocks - 1):
                    at = slice(b * width, (b + 1) * width)
                    res_ref[at, columns(c)] -= product((pth[q, at], ptl[q, at]), yq, NN)
                for b in range(blocks):
                    at = slice(b * width, (b + 1) * width)
                    grad[q, b] -= product(yq, (wh[c, at], wl[c, at]), NT)

            @pl.when((c == count // 2) & (p > 0))
            def _():
                chip_start(p - 1)

                @pl.when((p > 1) & (p < last))
                def _():
                    finish(p - 2)

        @pl.when(row == root)
        def _():
            inner = lax.broadcasted_iota(jnp.int32, (width, width), 0)
            within = lax.broadcasted_iota(jnp.int32, (width, width), 1)
            grad[p, blocks - 1] = jnp.where(inner >= within, grad[p, blocks - 1], 0.0)

        pair_start(p)

    chip_start(last)
    for p in range(last - 2, panels):
        finish(p)

    @pl.loop(0, panels)
    def _(p):
        root = n_row - 1 - p

        def act(g):
            for m in range(chips):
                pair_copy(p, m, g).wait_send()
            for j in range(1, chips):
                chip_copy(p, j, g).wait_send()

        groups(p, act)

        @pl.loop(0, count)
        def _(c):
            for h in range(HALVES):
                @pl.when((row >= root) & (row < n_row - 1) & ((p < last) | (row > last_root)))
                def _():
                    up(p, c, h).wait_send()

                @pl.when((row <= root) & (row > 0))
                def _():
                    down(p, c, h).wait_send()

    @pl.when(row == last_root)
    def _():
        @pl.loop(0, last)
        def _(p):
            far_panel(p).wait_send()

        @pl.loop(0, count)
        def _(c):
            far_rows(c).wait_send()


def store_kernel(res_ref, grad_ref, res_hbm, grad_hbm, sems):
    copies = (
        pltpu.make_async_copy(res_ref, res_hbm, sems.at[0]),
        pltpu.make_async_copy(grad_ref, grad_hbm, sems.at[1]),
    )
    for copy in copies:
        copy.start()
    for copy in copies:
        copy.wait()


def solution(mesh):
    n_row, n_col = mesh.shape["row"], mesh.shape["col"]

    def body(cotangent, whitened, panel_rows, diag_inverse):
        rows, rhs = cotangent.shape
        panels, width = diag_inverse.shape[:2]
        assert 3 <= panels <= n_row and n_col % 2 == 0
        count, blocks, part, chips = rhs // CHUNK, rows // width, width // n_col, n_col // 2
        vmem = pl.BlockSpec(memory_space=pltpu.VMEM)
        hbm = pl.BlockSpec(memory_space=pltpu.HBM)
        dma = pltpu.SemaphoreType.DMA
        kept = pl.pallas_call(
            functools.partial(kernel, n_row, n_col),
            out_shape=(pltpu.VMEM((rows, rhs), F32), pltpu.VMEM((panels, part, rows), F32)),
            in_specs=[hbm] * 4,
            out_specs=(vmem, vmem),
            scratch_shapes=[
                pltpu.VMEM((rows, rhs), F32),
                pltpu.VMEM((panels, width, rows), F32),
                pltpu.VMEM((panels, width, width), F32),
                pltpu.VMEM((panels, count, width, CHUNK), F32),
                pltpu.VMEM((panels, rows, width), BF16),
                pltpu.VMEM((panels, rows, width), BF16),
                pltpu.VMEM((panels, width, width), BF16),
                pltpu.VMEM((panels, width, width), BF16),
                pltpu.VMEM((count, rows, CHUNK), BF16),
                pltpu.VMEM((count, rows, CHUNK), BF16),
                pltpu.VMEM((panels, blocks, width, width), F32),
                pltpu.VMEM((panels, chips, blocks, part, width), F32),
                pltpu.VMEM((panels, chips, blocks, part, width), F32),
                pltpu.VMEM((panels - 1, width, width), F32),
                pltpu.VMEM((count, width, CHUNK), F32),
                pltpu.VMEM((count, width, CHUNK), F32),
                pltpu.VMEM((width, width), BF16),
                pltpu.VMEM((width, width), BF16),
                dma((5,)),
                dma((panels, count, HALVES)),
                dma((panels, count, HALVES)),
                dma((panels, count, HALVES)),
                dma((panels, chips, 2)),
                dma((panels, chips, 2)),
                dma((panels, chips, 2)),
                dma((panels, chips, 2)),
                dma((panels - 1,)),
                dma((panels - 1,)),
                dma((count,)),
                dma((count,)),
            ],
            compiler_params=pltpu.CompilerParams(
                collective_id=0, has_side_effects=True, vmem_limit_bytes=117 * 512 * 1024
            ),
        )(cotangent, whitened, panel_rows, diag_inverse)
        return pl.pallas_call(
            store_kernel,
            out_shape=tuple(jax.ShapeDtypeStruct(k.shape, F32) for k in kept),
            in_specs=[pl.BlockSpec(memory_space=pl.ANY)] * 2,
            out_specs=(hbm, hbm),
            scratch_shapes=[dma((2,))],
            compiler_params=pltpu.CompilerParams(vmem_limit_bytes=1024 * 1024),
        )(*kept)

    return jax.shard_map(
        body,
        mesh=mesh,
        in_specs=(P("row", "col"), P("row", "col"), P(None, None, "row"), P()),
        out_specs=(P("row", "col"), P(None, "col", "row")),
        check_vma=False,
    )
```
